1024 devices in a mesh: pipe: 16 (over y, core), expert: 64 (over x, z).
Axes of the slice: x: 4, y: 8, z: 16, core: 2. Of those that a mesh axis runs over, the one named last changes fastest.
Arguments:
- grad_sent: bfloat16 [16, 8192, 2048], P('pipe', 'expert'), may hold values from -6 to 6
- routes: int32 [16, 8192, 2], P('pipe', 'expert'), may hold values from 0 to 63, all different within a row; in each aligned block of 64 rows (0 to 63, 64 to 127, ..., all dimensions but the last counted through in order) at most 3 rows name the same one
- router_probs: float32 [16, 8192, 64], P('pipe', 'expert'), may hold values from 0.003125 to 0.078125
- saved_hidden: bfloat16 [16, 24576, 768], P('pipe', 'expert'), may hold values from -6 to 6
- w_down: bfloat16 [64, 768, 2048], P('expert'), may hold values from -0.21875 to 0.21875
- w_router: bfloat16 [2048, 64], replicated, may hold values from -0.125 to 0.125
Outputs:
- d_hidden: bfloat16 [16, 24576, 768], P('pipe', 'expert')
- grad_router_in: bfloat16 [16, 8192, 2048], P('pipe', 'expert')
The draws below stay inside these ranges and needn't reach their ends.
Inputs may be any that keep to these rules, and one draw needn't show every extreme that they name: `routes`: each token names 2 different experts. In each micro-batch of one device (an aligned block of 64 rows) no expert is named by more than 3 tokens, a bound that some block reaches.
All inputs are finite; a program needn't handle non-finite values.
Results may differ from the reference program's by a relative error of at most 0.0046.
Values may be sent and summed in bfloat16 or wider, within the bound.
A program may use at most 32 MiB of HBM per device.

```python
import math
import jax
import jax.numpy as jnp
import numpy as np
from jax import lax

D = 2048
FF = 768
TOP = 2
MICRO = 2
MB_TOK = 64
SECTIONS = 16
EXPERTS = 64
TOKENS = 8192
CAP = 3
SLOTS = 384


def shard_levels(stream_key, dims, shards, low, largest):
    gain, own = 1.0, jax.random.fold_in(stream_key, 6)
    for axis_at, blocks in shards:
        heights = jnp.exp(jax.random.uniform(jax.random.fold_in(own, axis_at), (blocks,), jnp.float32, low / len(shards), largest / len(shards)))
        gain = gain * jnp.repeat(heights, dims[axis_at] // blocks).reshape([-1 if axis == axis_at else 1 for axis in range(len(dims))])
    return gain


def shared_out(key, own, number, rows, amount, top, reach, lean):
    ranking = jax.random.permutation(key, amount)
    packed, usual = load_shares(amount, rows * top, reach, lean, True), load_shares(amount, rows * top, reach, lean, False)
    places = jnp.arange(amount)

    def named(sizes, turn):
        used = int((sizes > 0).sum())
        fixed = max(1, used // 4)
        shifted = fixed + (places - fixed + turn * (used - fixed)) % max(1, amount - fixed)
        return jnp.zeros((amount,), jnp.int32).at[ranking[jnp.where(places < fixed, places, shifted)]].set(jnp.asarray(sizes, jnp.int32))

    sizes = jnp.where(number % 4 == 0, named(packed, number // 4), named(usual, number - number // 4 - 1))
    mixed = jax.random.permutation(jax.random.fold_in(own, 3), amount)
    source_of, sink = mixed[0:amount // 2 * 2:2], mixed[1:amount // 2 * 2:2]
    slack = jnp.minimum(sizes[source_of] - 1, reach - sizes[sink]) // 2
    slack = jnp.where((source_of == ranking[0]) | (sink == ranking[0]) | (sizes[sink] == 0), 0, jnp.maximum(slack, 0))
    shifted = jax.random.randint(jax.random.fold_in(own, 4), (amount // 2,), 0, 1 << 20) % (slack + 1)
    sizes = sizes.at[source_of].add(-shifted).at[sink].add(shifted)
    items = jnp.searchsorted(jnp.cumsum(sizes), jnp.arange(rows * top), side="right").astype(jnp.int32)
    grid = items.reshape(top, rows).T
    grid = grid[jax.random.permutation(jax.random.fold_in(own, 1), rows)]
    turn = jax.random.randint(jax.random.fold_in(own, 2), (rows, 1), 0, top)
    return jnp.take_along_axis(grid, (jnp.arange(top)[None, :] + turn) % top, axis=1)


def load_shares(amount, total, limit, lean, full):
    loads = [(1 << 20) // math.isqrt(rank ** lean) + 1 for rank in range(1, amount + 1)]
    largest = limit if full else min(limit, max(-(-total // amount), total * loads[0] // sum(loads)))
    least = 1 if total - largest >= amount - 1 else 0
    counts, spare = [largest] + [least] * (amount - 1), total - largest - least * (amount - 1)
    while spare > 0:
        free = [i for i in range(1, amount) if counts[i] < largest] or [i for i in range(1, amount) if counts[i] < limit]
        whole, left = sum([loads[i] for i in free]), spare
        for i in free:
            addition = min(limit - counts[i], max(1, left * loads[i] // whole), spare)
            counts[i] = counts[i] + addition
            spare = spare - addition
    return np.array(counts)


def bell_draw(stream_key, extent, deviation, limit, cuts=(), held_as=jnp.bfloat16):
    loudness = shard_levels(stream_key, extent, cuts, -0.22, 0.18) if cuts else 1.0
    array = jax.random.normal(stream_key, extent, jnp.float32) * deviation * loudness
    return jnp.minimum(jnp.maximum(array, -limit), limit).astype(held_as)


def setup_inputs(seed: int = 0) -> dict:
    key_list = jax.random.split(jax.random.key(seed), 7)
    grad_sent = bell_draw(key_list[0], (SECTIONS, TOKENS, D), 1.0, 6.0, ((0, 16), (1, 64)))
    routes_keys = jax.random.split(jax.random.fold_in(key_list[1], 1), SECTIONS * TOKENS // MB_TOK)
    routes_turns = jax.random.permutation(jax.random.fold_in(key_list[1], 3), SECTIONS * TOKENS // MB_TOK)
    routes = jax.vmap(lambda own, number: shared_out(jax.random.fold_in(key_list[1], 2), own, number, MB_TOK, EXPERTS, TOP, CAP, 2))(routes_keys, routes_turns).reshape((SECTIONS, TOKENS, TOP))
    router_probs = jnp.clip(jnp.exp(math.log(0.078125) - 3.218876 * jax.random.uniform(key_list[2], (SECTIONS, TOKENS, EXPERTS), jnp.float32) ** shard_levels(key_list[2], (SECTIONS, TOKENS, EXPERTS), ((0, 16), (1, 64)), -0.2, 0.2)), 0.003125, 0.078125)
    saved_hidden = bell_draw(key_list[3], (SECTIONS, EXPERTS * SLOTS, FF), 1.0, 6.0, ((0, 16), (1, 64)))
    w_down = bell_draw(key_list[4], (EXPERTS, FF, D), FF ** -0.5, 0.21875, ((0, 64),))
    w_router = bell_draw(key_list[5], (D, EXPERTS), D ** -0.5, 0.125)
    return {"grad_sent": grad_sent, "routes": routes, "router_probs": router_probs, "saved_hidden": saved_hidden, "w_down": w_down, "w_router": w_router}


def reference(grad_sent, routes, router_probs, saved_hidden, w_down, w_router):
    incoming = jnp.roll(grad_sent, -1, axis=0)
    chosen = jnp.take_along_axis(router_probs, routes, axis=2)
    weights = chosen / jnp.sum(chosen, axis=2, keepdims=True)
    rounded = lax.optimization_barrier(weights.astype(jnp.bfloat16)).astype(jnp.float32)
    route_rows = routes.reshape(SECTIONS, EXPERTS, MICRO, MB_TOK * TOP)
    onehot = (route_rows[..., None] == jnp.arange(EXPERTS, dtype=jnp.int32)).astype(jnp.int32)
    rank_of = jnp.sum((jnp.cumsum(onehot, axis=3) - onehot) * onehot, axis=4).astype(jnp.int32)
    source = jnp.arange(EXPERTS, dtype=jnp.int32)[None, :, None, None]
    micro_step = jnp.arange(MICRO, dtype=jnp.int32)[None, None, :, None]
    position = route_rows * SLOTS + (micro_step * EXPERTS + source) * CAP + rank_of
    position = position.reshape(SECTIONS, TOKENS * TOP).astype(jnp.int32)
    weight_slots = rounded.reshape(SECTIONS, TOKENS * TOP)

    def one_section(pack):
        section_grad, slot_rows, slot_scales, held = pack
        spread = jnp.repeat(section_grad, TOP, axis=0)
        buffer = jnp.zeros((EXPERTS * SLOTS, D), jnp.bfloat16).at[slot_rows].set(spread)
        scale_buf = jnp.zeros((EXPERTS * SLOTS,), jnp.float32).at[slot_rows].set(slot_scales)

        def one_expert(inner):
            dy_rows, saved_rows, weight = inner
            grad_hidden = jnp.dot(dy_rows, weight.T, preferred_element_type=jnp.float32)
            route_grad = jnp.sum(grad_hidden * saved_rows.astype(jnp.float32), axis=1)
            return grad_hidden, route_grad

        grad_hidden, route_grad = lax.map(one_expert, (buffer.reshape(EXPERTS, SLOTS, D), held.reshape(EXPERTS, SLOTS, FF), w_down))
        section_hidden = (scale_buf[:, None] * grad_hidden.reshape(EXPERTS * SLOTS, FF)).astype(jnp.bfloat16)
        return section_hidden, route_grad.reshape(EXPERTS * SLOTS)[slot_rows]

    d_hidden, slot_grad = lax.map(one_section, (incoming, position, weight_slots, saved_hidden))
    slot_grad = slot_grad.reshape(SECTIONS, TOKENS, TOP)
    centred = slot_grad - jnp.sum(weights * slot_grad, axis=2, keepdims=True)
    logit_part = weights * centred
    onehot_tok = (routes[..., None] == jnp.arange(EXPERTS, dtype=jnp.int32)).astype(jnp.float32)
    logit_grad = jnp.sum(logit_part[..., None] * onehot_tok, axis=2)
    grad_in = jnp.einsum("ste,de->std", logit_grad, w_router.astype(jnp.float32), precision=lax.Precision.HIGHEST)
    return d_hidden, grad_in.astype(jnp.bfloat16)
```

```python
import functools

import jax
import jax.numpy as jnp
from jax import lax
from jax.experimental import pallas as pl
from jax.experimental.pallas import tpu as pltpu
from jax.sharding import PartitionSpec as P

TOP = 2
MICRO = 2
CAP = 3
LANES = 128
F32 = jnp.float32
BF16 = jnp.bfloat16


def iota(shape, axis):
    return lax.broadcasted_iota(jnp.int32, shape, axis)


def dot(a, b, dims=((1,), (0,)), precision=None):
    return lax.dot_general(
        a, b, (dims, ((), ())), precision=precision, preferred_element_type=F32
    )


def kernel(
    columns,
    depth,
    routes_ref,
    probs_ref,
    router_ref,
    grad_ref,
    saved_hbm,
    weight_hbm,
    hidden_ref,
    grad_in_ref,
    incoming,
    pick,
    swap,
    send,
    recv,
    saved,
    weight,
    scale_send,
    scale_recv,
    partial,
    back_send,
    back_recv,
    load_sem,
    pipe_send,
    pipe_recv,
    send_sem,
    recv_sem,
    scale_send_sem,
    scale_recv_sem,
    back_send_sem,
    back_recv_sem,
):
    experts = columns * depth
    slab = depth * CAP
    tokens = incoming.shape[1]
    groups = incoming.shape[2] // LANES
    unit = groups * CAP
    pipes = lax.axis_size("pipe")
    stage = lax.axis_index("pipe")
    me = lax.axis_index("expert")
    column, level = me // depth, me % depth

    barrier = pltpu.get_barrier_semaphore()

    def greet(step, carry):
        pl.semaphore_signal(barrier, inc=1, device_id={"expert": (me + step) % experts})
        return carry

    lax.fori_loop(1, experts, greet, 0)
    for distance in (1, pipes - 1):
        pl.semaphore_signal(barrier, inc=1, device_id={"pipe": (stage + distance) % pipes})

    load_weight = pltpu.make_async_copy(weight_hbm.at[0], weight, load_sem.at[0])
    load_saved = pltpu.make_async_copy(saved_hbm.at[0], saved, load_sem.at[1])
    load_weight.start()
    load_saved.start()

    all_tokens = MICRO * tokens
    expert_row = iota((experts, all_tokens), 0)
    named = [(expert_row == routes_ref[k : k + 1, :]).astype(F32) for k in range(TOP)]
    probs = probs_ref[...]
    chosen = [jnp.sum(named[k] * probs, axis=0, keepdims=True) for k in range(TOP)]
    total = chosen[0] + chosen[1]
    weights = [chosen[k] / total for k in range(TOP)]
    before, after = iota((all_tokens, all_tokens), 0), iota((all_tokens, all_tokens), 1)
    earlier = (before < after) & ((before >= tokens) == (after >= tokens))
    seen = dot((named[0] + named[1]).astype(BF16), earlier.astype(F32).astype(BF16))
    rank = [jnp.sum(named[k] * seen, axis=0, keepdims=True) for k in range(TOP)]
    micro = (iota((1, all_tokens), 1) >= tokens).astype(F32)
    lane_row = iota((LANES, all_tokens), 0).astype(F32)
    slot = [(lane_row == micro * CAP + rank[k]).astype(F32) for k in range(TOP)]
    scales = sum(
        dot(
            named[k].astype(BF16),
            (slot[k] * weights[k].astype(BF16).astype(F32)).astype(BF16),
            ((1,), (1,)),
        )
        for k in range(TOP)
    )
    scale_send[...] = scales.reshape(experts, 1, LANES)
    row = [routes_ref[k : k + 1, :].astype(F32) * CAP + rank[k] for k in range(TOP)]
    for m in range(MICRO):
        here = iota((experts * CAP, tokens), 0).astype(F32)
        part = [row[k][:, m * tokens : (m + 1) * tokens] for k in range(TOP)]
        pick[m] = ((here == part[0]) | (here == part[1])).astype(F32).astype(BF16)

    size = slab * groups
    index = iota((size, 1), 0)
    outer = lax.shift_right_logical(index * ((1 << 16) // unit + 1), 16)
    inner = index - outer * unit
    third = lax.shift_right_logical(inner * ((1 << 16) // CAP + 1), 16)
    target = third * unit + outer * CAP + (inner - third * CAP)
    swap[...] = (iota((size, size), 1) == target).astype(F32).astype(BF16)

    pl.semaphore_wait(barrier, experts - 1 + 2)

    def pipe_copy(m):
        return pltpu.make_async_remote_copy(
            src_ref=grad_ref.at[0, pl.ds(m * tokens, tokens)],
            dst_ref=incoming.at[m],
            send_sem=pipe_send.at[m],
            recv_sem=pipe_recv.at[m],
            device_id={"pipe": (stage + pipes - 1) % pipes},
        )

    for m in range(MICRO):
        pipe_copy(m).start()

    def scale_copy(peer):
        return pltpu.make_async_remote_copy(
            src_ref=scale_send.at[peer],
            dst_ref=scale_recv.at[me],
            send_sem=scale_send_sem,
            recv_sem=scale_recv_sem,
            device_id={"expert": peer},
        )

    def scale_out(step, carry):
        scale_copy((me + step) % experts).start()
        return carry

    lax.fori_loop(1, experts, scale_out, 0)
    pltpu.make_async_copy(scale_send.at[me], scale_recv.at[me], scale_recv_sem).start()

    def row_copy(m, far, to):
        return pltpu.make_async_remote_copy(
            src_ref=send.at[m, far, to],
            dst_ref=recv.at[m, column, level],
            send_sem=send_sem.at[m, far],
            recv_sem=recv_sem.at[m, column],
            device_id={"expert": far * depth + to},
        )

    def hop(step):
        half = step // 2
        forward = depth // 2 - half
        backward = 2 * depth - (depth // 2 - 1 - half)
        return (level + jnp.where(step % 2 == 0, forward, backward)) % depth

    def fill(m, far):
        start = pl.multiple_of(far * slab, 16)
        rows = dot(pick[m, pl.ds(start, slab), :], incoming[m]).astype(BF16)
        stacked = jnp.concatenate(
            [rows[:, j * LANES : (j + 1) * LANES] for j in range(groups)], axis=0
        )
        mixed = dot(swap[...], stacked).astype(BF16)
        send[m, far] = mixed.reshape(depth, unit, LANES)

    for m in range(MICRO):
        pipe_copy(m).wait_recv()

        def spread(turn, carry):
            far = (column + turn) % columns
            fill(m, far)

            def out(step, inner_carry):
                row_copy(m, far, hop(step)).start()
                return inner_carry

            lax.fori_loop(0, jnp.where(turn == 0, depth - 1, depth), out, 0)
            return carry

        lax.fori_loop(0, columns, spread, 0)
        pltpu.make_async_copy(
            send.at[m, column, level], recv.at[m, column, level], recv_sem.at[m, column]
        ).start()

    load_weight.wait()
    load_saved.wait()
    pltpu.make_async_copy(scale_send, scale_recv, scale_recv_sem).wait()

    owner = iota((slab, depth), 0)
    holder = (
        lax.shift_right_logical(owner * ((1 << 16) // CAP + 1), 16) == iota((slab, depth), 1)
    ).astype(F32)
    line = iota((slab, LANES), 0)
    own_rank = line - lax.shift_right_logical(line * ((1 << 16) // CAP + 1), 16) * CAP
    holder_t = (
        iota((depth, slab), 0)
        == lax.shift_right_logical(iota((depth, slab), 1) * ((1 << 16) // CAP + 1), 16)
    ).astype(F32)

    def back_copy(peer):
        return pltpu.make_async_remote_copy(
            src_ref=back_send.at[peer],
            dst_ref=back_recv.at[me],
            send_sem=back_send_sem,
            recv_sem=back_recv_sem,
            device_id={"expert": peer},
        )

    for m in range(MICRO):
        ours = iota((slab, LANES), 1) == own_rank + m * CAP

        def gather(turn, carry):
            source = (column + columns - turn) % columns
            pltpu.make_async_copy(
                send.at[m, source], recv.at[m, source], recv_sem.at[m, source]
            ).wait()
            mixed = recv[m, source].reshape(size, LANES)
            rows = dot(swap[...], mixed).astype(BF16)
            flat = jnp.concatenate(
                [rows[j * slab : (j + 1) * slab] for j in range(groups)], axis=1
            )
            grad = dot(flat, weight[...], ((1,), (1,)))
            start = pl.multiple_of((m * columns + source) * slab, 16)
            held = saved[pl.ds(start, slab), :].astype(F32)
            route_grad = jnp.sum(grad * held, axis=1, keepdims=True)
            first = pl.multiple_of(source * depth, 16)
            all_scales = scale_recv[pl.ds(first, depth)].reshape(depth, LANES)
            spread_scales = dot(holder.astype(BF16), all_scales.astype(BF16))
            scale = jnp.sum(jnp.where(ours, spread_scales, 0.0), axis=1, keepdims=True)
            hidden_ref[0, pl.ds(start, slab), :] = (scale * grad).astype(BF16)
            sums = dot(
                holder_t, jnp.where(ours, route_grad, 0.0), precision=lax.Precision.HIGHEST
            )
            if m == 0:
                partial[pl.ds(first, depth), :] = sums
            else:
                both = partial[pl.ds(first, depth), :] + sums
                back_send[pl.ds(first, depth)] = both.reshape(depth, 1, LANES)

                def back(step, inner_carry):
                    back_copy(source * depth + hop(step)).start()
                    return inner_carry

                lax.fori_loop(0, jnp.where(turn == 0, depth - 1, depth), back, 0)
            return carry

        lax.fori_loop(0, columns, gather, 0)
    pltpu.make_async_copy(back_send.at[me], back_recv.at[me], back_recv_sem).start()

    for m in range(MICRO):
        pipe_copy(m).wait_send()

        def left(turn, carry):
            far = (column + turn) % columns
            pltpu.make_async_copy(send.at[m, far], recv.at[m, far], send_sem.at[m, far]).wait()
            return carry

        lax.fori_loop(1, columns, left, 0)
        pltpu.make_async_copy(
            send.at[m, column, pl.ds(0, depth - 1)],
            recv.at[m, column, pl.ds(0, depth - 1)],
            send_sem.at[m, column],
        ).wait()
    others = pl.ds(0, experts - 1)
    pltpu.make_async_copy(scale_send.at[others], scale_recv.at[others], scale_send_sem).wait()

    pltpu.make_async_copy(back_send, back_recv, back_recv_sem).wait()
    returned = back_recv[...].reshape(experts, LANES)
    slot_grad = [
        jnp.sum(
            slot[k] * dot(returned, named[k], ((0,), (0,)), lax.Precision.HIGHEST),
            axis=0,
            keepdims=True,
        )
        for k in range(TOP)
    ]
    mean = weights[0] * slot_grad[0] + weights[1] * slot_grad[1]
    logit = sum(named[k] * (weights[k] * (slot_grad[k] - mean)) for k in range(TOP))
    logit = logit.T
    high = logit.astype(BF16)
    low = (logit - high.astype(F32)).astype(BF16)
    router = router_ref[...]
    grad_in_ref[0] = (dot(high, router) + dot(low, router)).astype(BF16)
    pltpu.make_async_copy(back_send.at[others], back_recv.at[others], back_send_sem).wait()


def solution(mesh):
    experts = mesh.shape["expert"]

    def on_device(grad_sent, routes, router_probs, saved_hidden, w_down, w_router):
        model_width = grad_sent.shape[2]
        slots, width = saved_hidden.shape[1:]
        tokens = routes.shape[1] // MICRO
        depth = model_width // LANES
        columns = experts // depth
        slab = depth * CAP
        unit = depth * CAP
        in_vmem = pl.BlockSpec(memory_space=pltpu.VMEM)
        in_place = pl.BlockSpec(memory_space=pl.ANY)
        return pl.pallas_call(
            functools.partial(kernel, columns, depth),
            out_shape=(
                jax.ShapeDtypeStruct((1, slots, width), BF16),
                jax.ShapeDtypeStruct((1, MICRO * tokens, model_width), BF16),
            ),
            in_specs=[in_vmem, in_vmem, in_vmem, in_place, in_place, in_place],
            out_specs=(in_vmem, in_vmem),
            scratch_shapes=[
                pltpu.VMEM((MICRO, tokens, model_width), BF16),
                pltpu.VMEM((MICRO, experts * CAP, tokens), BF16),
                pltpu.VMEM((slab * depth, slab * depth), BF16),
                pltpu.VMEM((MICRO, columns, depth, unit, LANES), BF16),
                pltpu.VMEM((MICRO, columns, depth, unit, LANES), BF16),
                pltpu.VMEM((slots, width), BF16),
                pltpu.VMEM((width, model_width), BF16),
                pltpu.VMEM((experts, 1, LANES), F32),
                pltpu.VMEM((experts, 1, LANES), F32),
                pltpu.VMEM((experts, LANES), F32),
                pltpu.VMEM((experts, 1, LANES), F32),
                pltpu.VMEM((experts, 1, LANES), F32),
                pltpu.SemaphoreType.DMA((2,)),
                pltpu.SemaphoreType.DMA((MICRO,)),
                pltpu.SemaphoreType.DMA((MICRO,)),
                pltpu.SemaphoreType.DMA((MICRO, columns)),
                pltpu.SemaphoreType.DMA((MICRO, columns)),
                pltpu.SemaphoreType.DMA,
                pltpu.SemaphoreType.DMA,
                pltpu.SemaphoreType.DMA,
                pltpu.SemaphoreType.DMA,
            ],
            compiler_params=pltpu.CompilerParams(
                collective_id=0, has_side_effects=True, vmem_limit_bytes=48 << 20
            ),
            name="routed_backward",
        )(routes[0].T, router_probs[0].T, w_router.T, grad_sent, saved_hidden, w_down)

    placed = (
        P("pipe", "expert", None),
        P("pipe", "expert", None),
        P("pipe", "expert", None),
        P("pipe", "expert", None),
        P("expert", None, None),
        P(),
    )
    return jax.shard_map(
        on_device,
        mesh=mesh,
        in_specs=placed,
        out_specs=(P("pipe", "expert", None), P("pipe", "expert", None)),
        check_vma=False,
    )
```

```python
import functools

import jax
import jax.numpy as jnp
from jax import lax
from jax.experimental import pallas as pl
from jax.experimental.pallas import tpu as pltpu
from jax.sharding import PartitionSpec as P

TOP = 2
MICRO = 2
CAP = 3
EACH = MICRO * CAP
NEAR = 3
LANES = 128
F32 = jnp.float32
BF16 = jnp.bfloat16


def iota(shape, axis):
    return lax.broadcasted_iota(jnp.int32, shape, axis)


def split(index, size):
    outer = lax.shift_right_logical(index * ((1 << 16) // size + 1), 16)
    return outer, index - outer * size


def onehot(condition):
    return condition.astype(F32).astype(BF16)


def dot(a, b, dims=((1,), (0,)), precision=None):
    return lax.dot_general(
        a, b, (dims, ((), ())), precision=precision, preferred_element_type=F32
    )


def kernel(
    columns,
    depth,
    routes_hbm,
    probs_hbm,
    router_hbm,
    grad_hbm,
    saved_hbm,
    weight_hbm,
    hidden_hbm,
    grad_in_hbm,
    routes_ref,
    probs_ref,
    router_ref,
    incoming,
    pick,
    order,
    place,
    apart,
    together,
    send,
    recv,
    saved,
    weight,
    scale_send,
    scale_recv,
    hidden,
    placed,
    grad_in,
    back_send,
    back_recv,
    load_sem,
    store_sem,
    pipe_send,
    pipe_recv,
    send_sem,
    recv_sem,
    scale_send_sem,
    scale_recv_sem,
    back_send_sem,
    back_recv_sem,
    column_ready,
    level_ready,
):
    experts = columns * depth
    half = depth // 2
    near = min(NEAR, half - 1)
    peers = 2 * columns
    rows = peers * EACH
    slots = half * rows
    tokens = incoming.shape[0] // MICRO
    all_tokens = MICRO * tokens
    groups = incoming.shape[1] // LANES
    unit = groups * EACH
    size = peers * unit
    pipes = lax.axis_size("pipe")
    stage = lax.axis_index("pipe")
    me = lax.axis_index("expert")
    column, level = me // depth, me % depth

    def expert_at(x, z):
        return (x % columns) * depth + z % depth

    beside = [{"expert": expert_at(column + step, level)} for step in (1, columns - 1)]
    along = [{"expert": expert_at(column, level + step)} for step in (1, depth - 1)]
    behind = {"pipe": (stage + pipes - 1) % pipes}
    ahead = {"pipe": (stage + 1) % pipes}

    barrier = pltpu.get_barrier_semaphore()
    for device in along + beside + [behind, ahead]:
        pl.semaphore_signal(barrier, inc=1, device_id=device)
    loads = [
        pltpu.make_async_copy(source, target, load_sem.at[at])
        for at, (source, target) in enumerate(
            (
                (routes_hbm, routes_ref),
                (probs_hbm, probs_ref),
                (saved_hbm.at[0], saved),
                (weight_hbm.at[0], weight),
                (router_hbm, router_ref),
            )
        )
    ]
    for load in loads:
        load.start()
    pl.semaphore_wait(barrier, 6)

    pipe_copy = pltpu.make_async_remote_copy(
        src_ref=grad_hbm.at[0],
        dst_ref=incoming,
        send_sem=pipe_send,
        recv_sem=pipe_recv,
        device_id=behind,
    )
    pipe_copy.start()
    for device in beside:
        pl.semaphore_signal(column_ready, inc=1, device_id=device)

    loads[0].wait()
    loads[1].wait()
    expert_row = iota((experts, all_tokens), 0)
    named = [(expert_row == routes_ref[k : k + 1, :]).astype(F32) for k in range(TOP)]
    probs = probs_ref[...]
    chosen = [jnp.sum(named[k] * probs, axis=0, keepdims=True) for k in range(TOP)]
    total = chosen[0] + chosen[1]
    weights = [chosen[k] / total for k in range(TOP)]
    before, after = iota((all_tokens, all_tokens), 0), iota((all_tokens, all_tokens), 1)
    earlier = (before < after) & ((before >= tokens) == (after >= tokens))
    seen = dot((named[0] + named[1]).astype(BF16), onehot(earlier))
    micro = (iota((1, all_tokens), 1) >= tokens).astype(F32)
    within = [
        micro * CAP + jnp.sum(named[k] * seen, axis=0, keepdims=True) for k in range(TOP)
    ]
    lane_row = iota((LANES, all_tokens), 0).astype(F32)
    slot = [(lane_row == within[k]).astype(F32) for k in range(TOP)]
    goal = [routes_ref[k : k + 1, :].astype(F32) * EACH + within[k] for k in range(TOP)]

    pl.semaphore_wait(column_ready, 2)

    def tell(step):
        for device in along:
            pl.semaphore_signal(level_ready.at[step], inc=1, device_id=device)

    tell(0)

    def levels(wave, sign):
        apart_by = jnp.where(wave == 0, half, wave)
        first = level + depth + sign * wave
        second = level + depth - sign * apart_by
        return first, second

    def peer_of(wave, peer, sign):
        first, second = levels(wave, sign)
        other = (peer >= columns).astype(jnp.int32)
        z = jnp.where(other == 1, second, first)
        z = z - jnp.where(z >= 2 * depth, 2 * depth, jnp.where(z >= depth, depth, 0))
        return (peer - other * columns) * depth + z

    def natural(index):
        wave, rest = split(index, rows)
        peer, each = split(rest, EACH)
        m, rank = split(each, CAP)
        return (m * experts + peer_of(wave, peer, -1)) * CAP + rank

    index = iota((slots, 1), 0)
    wave, rest = split(index, rows)
    peer, each = split(rest, EACH)
    wanted = (peer_of(wave, peer, 1) * EACH + each).astype(F32)
    pick[...] = onehot((wanted == goal[0]) | (wanted == goal[1]))
    order[...] = onehot(iota((slots, slots), 1) == natural(index))
    place[...] = onehot(iota((slots, slots), 0) == natural(iota((1, slots), 1)))
    line = iota((size, 1), 0)
    p, inner = split(line, unit)
    j, c = split(inner, EACH)
    apart[...] = onehot(iota((size, size), 1) == j * rows + p * EACH + c)
    j, inner = split(line, rows)
    p, c = split(inner, EACH)
    together[...] = onehot(iota((size, size), 1) == p * unit + j * EACH + c)
    scales = sum(
        dot(
            named[k].astype(BF16),
            (slot[k] * weights[k].astype(BF16).astype(F32)).astype(BF16),
            ((1,), (1,)),
        )
        for k in range(TOP)
    )
    wave, peer = split(iota((half * peers, 1), 0), peers)
    turned = onehot(iota((half * peers, experts), 1) == peer_of(wave, peer, 1))
    scale_send[...] = dot(turned, scales.astype(BF16)).reshape(half, peers, 1, LANES)

    def hear(step, carry):
        pl.semaphore_wait(level_ready.at[step], 2)
        tell(step + 1)
        return carry

    lax.fori_loop(0, near, hear, 0)
    pipe_copy.wait_recv()

    def wave_at(turn):
        return jnp.where(turn < near, turn + 1, jnp.where(turn == near, 0, half + near - turn))

    def visit(wave, sign, step):
        first, second = levels(wave, sign)
        other = step % 2
        x = (column + step // 2) % columns
        return other * columns + x, other * columns + column, expert_at(
            x, jnp.where(other == 1, second, first)
        )

    def row_copy(wave, step):
        there, here, device = visit(wave, 1, step)
        return pltpu.make_async_remote_copy(
            src_ref=send.at[wave, there],
            dst_ref=recv.at[wave, here],
            send_sem=send_sem.at[wave],
            recv_sem=recv_sem.at[wave],
            device_id={"expert": device},
        )

    def scale_copy(wave, step):
        there, here, device = visit(wave, 1, step)
        return pltpu.make_async_remote_copy(
            src_ref=scale_send.at[wave, there],
            dst_ref=scale_recv.at[wave, here],
            send_sem=scale_send_sem.at[wave],
            recv_sem=scale_recv_sem.at[wave],
            device_id={"expert": device},
        )

    def back_copy(wave, step):
        there, _, device = visit(wave, -1, step)
        return pltpu.make_async_remote_copy(
            src_ref=back_send.at[wave, there],
            dst_ref=back_recv.at[me],
            send_sem=back_send_sem,
            recv_sem=back_recv_sem,
            device_id={"expert": device},
        )

    def spread(turn, carry):
        wave = wave_at(turn)
        start = pl.multiple_of(wave * rows, 16)
        picked = dot(pick[pl.ds(start, rows), :], incoming[...]).astype(BF16)
        stacked = jnp.concatenate(
            [picked[:, j * LANES : (j + 1) * LANES] for j in range(groups)], axis=0
        )
        send[wave] = dot(apart[...], stacked).astype(BF16).reshape(peers, unit, LANES)
        others = jnp.where(wave == 0, 1, 0)

        def out(step, inner_carry):
            scale_copy(wave, step).start()
            row_copy(wave, step).start()
            return inner_carry

        lax.fori_loop(others, peers, out, 0)
        return carry

    lax.fori_loop(0, near, spread, 0)

    def hear_last(step, carry):
        hear(step, carry)
        return carry

    lax.fori_loop(near, half - 1, hear_last, 0)
    pl.semaphore_wait(level_ready.at[half - 1], 2)
    lax.fori_loop(near, half, spread, 0)
    pltpu.make_async_copy(scale_send.at[0, column], scale_recv.at[0, column], scale_recv_sem.at[0]).start()
    pltpu.make_async_copy(send.at[0, column], recv.at[0, column], recv_sem.at[0]).start()

    loads[2].wait()
    loads[3].wait()
    line_peer, line_slot = split(iota((rows, LANES), 0), EACH)
    ours = iota((rows, LANES), 1) == line_slot
    holder = onehot(split(iota((rows, peers), 0), EACH)[0] == iota((rows, peers), 1))
    holder_t = (split(iota((peers, rows), 1), EACH)[0] == iota((peers, rows), 0)).astype(F32)

    def gather(turn, carry):
        wave = wave_at(turn)
        start = pl.multiple_of(wave * rows, 16)
        held = dot(order[pl.ds(start, rows), :], saved[...])
        pltpu.make_async_copy(scale_send.at[wave], scale_recv.at[wave], scale_recv_sem.at[wave]).wait()
        all_scales = scale_recv[wave].reshape(peers, LANES).astype(BF16)
        scale = jnp.sum(jnp.where(ours, dot(holder, all_scales), 0.0), axis=1, keepdims=True)
        pltpu.make_async_copy(send.at[wave], recv.at[wave], recv_sem.at[wave]).wait()
        mixed = dot(together[...], recv[wave].reshape(size, LANES)).astype(BF16)
        flat = jnp.concatenate(
            [mixed[j * rows : (j + 1) * rows] for j in range(groups)], axis=1
        )
        grad = dot(flat, weight[...], ((1,), (1,)))
        route_grad = jnp.sum(grad * held, axis=1, keepdims=True)
        sums = dot(holder_t, jnp.where(ours, route_grad, 0.0), precision=lax.Precision.HIGHEST)
        back_send[wave] = sums.reshape(peers, 1, LANES)
        others = jnp.where(wave == 0, 1, 0)

        def back(step, inner_carry):
            back_copy(wave, step).start()
            return inner_carry

        lax.fori_loop(others, peers, back, 0)
        hidden[pl.ds(start, rows), :] = (scale * grad).astype(BF16)
        return carry

    lax.fori_loop(0, half, gather, 0)
    pltpu.make_async_copy(back_send.at[0, column], back_recv.at[me], back_recv_sem).start()
    placed[...] = dot(place[...], hidden[...]).astype(BF16)
    store_hidden = pltpu.make_async_copy(placed, hidden_hbm.at[0], store_sem.at[0])
    store_hidden.start()

    pipe_copy.wait_send()

    def left(wave, carry):
        pltpu.make_async_copy(send.at[wave], recv.at[wave], send_sem.at[wave]).wait()
        pltpu.make_async_copy(scale_send.at[wave], scale_recv.at[wave], scale_send_sem.at[wave]).wait()
        return carry

    lax.fori_loop(1, half, left, 0)
    remote = pl.ds(0, peers - 1)
    pltpu.make_async_copy(send.at[0, remote], recv.at[0, remote], send_sem.at[0]).wait()
    pltpu.make_async_copy(scale_send.at[0, remote], scale_recv.at[0, remote], scale_send_sem.at[0]).wait()
    loads[4].wait()

    pltpu.make_async_copy(back_recv, back_recv, back_recv_sem).wait()
    returned = back_recv[...].reshape(experts, LANES)
    slot_grad = [
        jnp.sum(
            slot[k] * dot(returned, named[k], ((0,), (0,)), lax.Precision.HIGHEST),
            axis=0,
            keepdims=True,
        )
        for k in range(TOP)
    ]
    mean = weights[0] * slot_grad[0] + weights[1] * slot_grad[1]
    logit = sum(named[k] * (weights[k] * (slot_grad[k] - mean)) for k in range(TOP))
    logit = logit.T
    high = logit.astype(BF16)
    low = (logit - high.astype(F32)).astype(BF16)
    router = router_ref[...]
    grad_in[...] = (dot(high, router) + dot(low, router)).astype(BF16)
    store_grad = pltpu.make_async_copy(grad_in, grad_in_hbm.at[0], store_sem.at[1])
    store_grad.start()
    others = pl.ds(0, experts - 1)
    pltpu.make_async_copy(back_recv.at[others], back_recv.at[others], back_send_sem).wait()
    store_hidden.wait()
    store_grad.wait()


def solution(mesh):
    experts = mesh.shape["expert"]
    depth = 16 if experts % 16 == 0 else 4

    def on_device(grad_sent, routes, router_probs, saved_hidden, w_down, w_router):
        all_tokens, model_width = grad_sent.shape[1:]
        slots, width = saved_hidden.shape[1:]
        columns = experts // depth
        half = depth // 2
        peers = 2 * columns
        unit = model_width // LANES * EACH
        in_place = pl.BlockSpec(memory_space=pl.ANY)
        dma = pltpu.SemaphoreType.DMA
        return pl.pallas_call(
            functools.partial(kernel, columns, depth),
            out_shape=(
                jax.ShapeDtypeStruct((1, slots, width), BF16),
                jax.ShapeDtypeStruct((1, all_tokens, model_width), BF16),
            ),
            in_specs=[in_place] * 6,
            out_specs=(in_place, in_place),
            scratch_shapes=[
                pltpu.VMEM((TOP, all_tokens), jnp.int32),
                pltpu.VMEM((experts, all_tokens), F32),
                pltpu.VMEM((experts, model_width), BF16),
                pltpu.VMEM((all_tokens, model_width), BF16),
                pltpu.VMEM((slots, all_tokens), BF16),
                pltpu.VMEM((slots, slots), BF16),
                pltpu.VMEM((slots, slots), BF16),
                pltpu.VMEM((peers * unit, peers * unit), BF16),
                pltpu.VMEM((peers * unit, peers * unit), BF16),
                pltpu.VMEM((half, peers, unit, LANES), BF16),
                pltpu.VMEM((half, peers, unit, LANES), BF16),
                pltpu.VMEM((slots, width), BF16),
                pltpu.VMEM((width, model_width), BF16),
                pltpu.VMEM((half, peers, 1, LANES), F32),
                pltpu.VMEM((half, peers, 1, LANES), F32),
                pltpu.VMEM((slots, width), BF16),
                pltpu.VMEM((slots, width), BF16),
                pltpu.VMEM((all_tokens, model_width), BF16),
                pltpu.VMEM((half, peers, 1, LANES), F32),
                pltpu.VMEM((experts, 1, LANES), F32),
                dma((5,)),
                dma((2,)),
                dma,
                dma,
                dma((half,)),
                dma((half,)),
                dma((half,)),
                dma((half,)),
                dma,
                dma,
                pltpu.SemaphoreType.REGULAR,
                pltpu.SemaphoreType.REGULAR((half,)),
            ],
            compiler_params=pltpu.CompilerParams(
                collective_id=0, has_side_effects=True, vmem_limit_bytes=67043328
            ),
            name="routed_backward",
        )(routes[0].T, router_probs[0].T, w_router.T, grad_sent, saved_hidden, w_down)

    placed = (
        P("pipe", "expert", None),
        P("pipe", "expert", None),
        P("pipe", "expert", None),
        P("pipe", "expert", None),
        P("expert", None, None),
        P(),
    )
    return jax.shard_map(
        on_device,
        mesh=mesh,
        in_specs=placed,
        out_specs=(P("pipe", "expert", None), P("pipe", "expert", None)),
        check_vma=False,
    )
```

```python
import functools

import jax
import jax.numpy as jnp
from jax import lax
from jax.experimental import pallas as pl
from jax.experimental.pallas import tpu as pltpu
from jax.sharding import PartitionSpec as P

TOP = 2
MICRO = 2
CAP = 3
LANES = 128
F32 = jnp.float32
BF16 = jnp.bfloat16


def iota(shape, axis):
    return lax.broadcasted_iota(jnp.int32, shape, axis)


def split(index, size):
    outer = lax.shift_right_logical(index * ((1 << 16) // size + 1), 16)
    return outer, index - outer * size


def onehot(condition):
    return condition.astype(F32).astype(BF16)


def dot(a, b, dims=((1,), (0,)), precision=None):
    return lax.dot_general(
        a, b, (dims, ((), ())), precision=precision, preferred_element_type=F32
    )


def kernel(
    columns,
    depth,
    routes_hbm,
    probs_hbm,
    grad_hbm,
    saved_hbm,
    weight_hbm,
    hidden_hbm,
    logit_ref,
    routes_ref,
    probs_ref,
    incoming,
    pick,
    swap,
    send,
    recv,
    saved,
    weight,
    scale_send,
    scale_recv,
    partial,
    hidden,
    back_send,
    back_recv,
    load_sem,
    store_sem,
    pipe_send,
    pipe_recv,
    send_sem,
    recv_sem,
    scale_send_sem,
    scale_recv_sem,
    back_send_sem,
    back_recv_sem,
    column_ready,
    level_ready,
):
    experts = columns * depth
    slab = depth * CAP
    tokens = incoming.shape[1]
    groups = incoming.shape[2] // LANES
    unit = groups * CAP
    size = slab * groups
    pipes = lax.axis_size("pipe")
    stage = lax.axis_index("pipe")
    me = lax.axis_index("expert")
    column, level = me // depth, me % depth

    def expert_at(x, z):
        return {"expert": (x % columns) * depth + z % depth}

    def along(distance):
        return [expert_at(column, level + step) for step in (distance, depth - distance)]

    beside = [expert_at(column + step, level) for step in (1, columns - 1)]
    behind = {"pipe": (stage + pipes - 1) % pipes}
    ahead = {"pipe": (stage + 1) % pipes}

    barrier = pltpu.get_barrier_semaphore()
    for device in along(1) + beside + [behind, ahead]:
        pl.semaphore_signal(barrier, inc=1, device_id=device)
    loads = [
        pltpu.make_async_copy(source, target, load_sem.at[at])
        for at, (source, target) in enumerate(
            (
                (routes_hbm, routes_ref),
                (probs_hbm, probs_ref),
                (saved_hbm.at[0], saved),
                (weight_hbm.at[0], weight),
            )
        )
    ]
    for load in loads:
        load.start()
    pl.semaphore_wait(barrier, 6)

    def pipe_copy(m):
        return pltpu.make_async_remote_copy(
            src_ref=grad_hbm.at[0, pl.ds(m * tokens, tokens)],
            dst_ref=incoming.at[m],
            send_sem=pipe_send.at[m],
            recv_sem=pipe_recv.at[m],
            device_id=behind,
        )

    for m in range(MICRO):
        pipe_copy(m).start()
    for device in beside:
        pl.semaphore_signal(column_ready, inc=1, device_id=device)

    loads[0].wait()
    loads[1].wait()
    all_tokens = MICRO * tokens
    expert_row = iota((experts, all_tokens), 0)
    named = [(expert_row == routes_ref[k : k + 1, :]).astype(F32) for k in range(TOP)]
    probs = probs_ref[...]
    chosen = [jnp.sum(named[k] * probs, axis=0, keepdims=True) for k in range(TOP)]
    total = chosen[0] + chosen[1]
    weights = [chosen[k] / total for k in range(TOP)]
    before, after = iota((all_tokens, all_tokens), 0), iota((all_tokens, all_tokens), 1)
    earlier = (before < after) & ((before >= tokens) == (after >= tokens))
    seen = dot((named[0] + named[1]).astype(BF16), onehot(earlier))
    rank = [jnp.sum(named[k] * seen, axis=0, keepdims=True) for k in range(TOP)]
    row = [routes_ref[k : k + 1, :].astype(F32) * CAP + rank[k] for k in range(TOP)]

    rounds = [1] + [1 << at for at in range(depth.bit_length() - 2)]

    def tell(at):
        for device in along(rounds[at]):
            pl.semaphore_signal(level_ready.at[at], inc=1, device_id=device)

    def hear(at):
        pl.semaphore_wait(level_ready.at[at], 2)

    pl.semaphore_wait(column_ready, 2)
    tell(0)
    for m in range(MICRO):
        here = iota((experts * CAP, tokens), 0).astype(F32)
        part = [row[k][:, m * tokens : (m + 1) * tokens] for k in range(TOP)]
        pick[m] = onehot((here == part[0]) | (here == part[1]))
    hear(0)
    tell(1)
    micro = (iota((1, all_tokens), 1) >= tokens).astype(F32)
    lane_row = iota((LANES, all_tokens), 0).astype(F32)
    slot = [(lane_row == micro * CAP + rank[k]).astype(F32) for k in range(TOP)]
    outer, inner = split(iota((size, 1), 0), unit)
    third, own = split(inner, CAP)
    swap[...] = onehot(iota((size, size), 1) == third * unit + outer * CAP + own)
    for at in range(1, len(rounds) - 1):
        hear(at)
        tell(at + 1)
    scales = sum(
        dot(
            named[k].astype(BF16),
            (slot[k] * weights[k].astype(BF16).astype(F32)).astype(BF16),
            ((1,), (1,)),
        )
        for k in range(TOP)
    )
    scale_send[...] = scales.reshape(experts, 1, LANES)

    def scale_copy(peer):
        return pltpu.make_async_remote_copy(
            src_ref=scale_send.at[peer],
            dst_ref=scale_recv.at[me],
            send_sem=scale_send_sem,
            recv_sem=scale_recv_sem,
            device_id={"expert": peer},
        )

    def scale_out(step, carry):
        scale_copy((me + step) % experts).start()
        return carry

    def row_copy(m, far, to):
        return pltpu.make_async_remote_copy(
            src_ref=send.at[m, far, to],
            dst_ref=recv.at[m, column, level],
            send_sem=send_sem.at[m, far],
            recv_sem=recv_sem.at[m, column],
            device_id={"expert": far * depth + to},
        )

    def hop(step):
        half = step // 2
        forward = depth // 2 - half
        backward = 2 * depth - (depth // 2 - 1 - half)
        return (level + jnp.where(step % 2 == 0, forward, backward)) % depth

    def fill(m, far):
        start = pl.multiple_of(far * slab, 16)
        rows = dot(pick[m, pl.ds(start, slab), :], incoming[m]).astype(BF16)
        stacked = jnp.concatenate(
            [rows[:, j * LANES : (j + 1) * LANES] for j in range(groups)], axis=0
        )
        mixed = dot(swap[...], stacked).astype(BF16)
        send[m, far] = mixed.reshape(depth, unit, LANES)

    def spread(m, first_step, last_step, packs):
        def body(turn, carry):
            far = (column + turn) % columns
            if packs:
                fill(m, far)

            def out(step, inner_carry):
                row_copy(m, far, hop(step)).start()
                return inner_carry

            end = last_step
            if last_step == depth:
                end = jnp.where(turn == 0, depth - 1, depth)
            lax.fori_loop(first_step, end, out, 0)
            return carry

        lax.fori_loop(0, columns, body, 0)

    def stay(m):
        pltpu.make_async_copy(
            send.at[m, column, level], recv.at[m, column, level], recv_sem.at[m, column]
        ).start()

    far_steps = depth // 2 - 1
    pipe_copy(0).wait_recv()
    spread(0, far_steps, depth, True)
    hear(len(rounds) - 1)
    spread(0, 0, far_steps, False)
    lax.fori_loop(1, experts, scale_out, 0)
    pltpu.make_async_copy(scale_send.at[me], scale_recv.at[me], scale_recv_sem).start()
    pipe_copy(1).wait_recv()
    spread(1, 0, depth, True)
    for m in range(MICRO):
        stay(m)

    loads[2].wait()
    loads[3].wait()
    pltpu.make_async_copy(scale_send, scale_recv, scale_recv_sem).wait()

    owner = iota((slab, depth), 0)
    holder = (
        lax.shift_right_logical(owner * ((1 << 16) // CAP + 1), 16) == iota((slab, depth), 1)
    ).astype(F32)
    line = iota((slab, LANES), 0)
    own_rank = line - lax.shift_right_logical(line * ((1 << 16) // CAP + 1), 16) * CAP
    holder_t = (
        iota((depth, slab), 0)
        == lax.shift_right_logical(iota((depth, slab), 1) * ((1 << 16) // CAP + 1), 16)
    ).astype(F32)

    def back_copy(peer):
        return pltpu.make_async_remote_copy(
            src_ref=back_send.at[peer],
            dst_ref=back_recv.at[me],
            send_sem=back_send_sem,
            recv_sem=back_recv_sem,
            device_id={"expert": peer},
        )

    for m in range(MICRO):
        ours = iota((slab, LANES), 1) == own_rank + m * CAP

        def gather(turn, carry):
            source = (column + columns - turn) % columns
            pltpu.make_async_copy(
                send.at[m, source], recv.at[m, source], recv_sem.at[m, source]
            ).wait()
            mixed = recv[m, source].reshape(size, LANES)
            rows = dot(swap[...], mixed).astype(BF16)
            flat = jnp.concatenate(
                [rows[j * slab : (j + 1) * slab] for j in range(groups)], axis=1
            )
            grad = dot(flat, weight[...], ((1,), (1,)))
            start = pl.multiple_of((m * columns + source) * slab, 16)
            held = saved[pl.ds(start, slab), :].astype(F32)
            route_grad = jnp.sum(grad * held, axis=1, keepdims=True)
            first = pl.multiple_of(source * depth, 16)
            all_scales = scale_recv[pl.ds(first, depth)].reshape(depth, LANES)
            spread_scales = dot(holder.astype(BF16), all_scales.astype(BF16))
            scale = jnp.sum(jnp.where(ours, spread_scales, 0.0), axis=1, keepdims=True)
            hidden[pl.ds(start, slab), :] = (scale * grad).astype(BF16)
            stored = pl.ds(start, slab)
            pltpu.make_async_copy(hidden.at[stored], hidden_hbm.at[stored], store_sem).start()
            sums = dot(
                holder_t, jnp.where(ours, route_grad, 0.0), precision=lax.Precision.HIGHEST
            )
            if m == 0:
                partial[pl.ds(first, depth), :] = sums
            else:
                both = partial[pl.ds(first, depth), :] + sums
                back_send[pl.ds(first, depth)] = both.reshape(depth, 1, LANES)

                def back(step, inner_carry):
                    back_copy(source * depth + hop(step)).start()
                    return inner_carry

                lax.fori_loop(0, jnp.where(turn == 0, depth - 1, depth), back, 0)
            return carry

        lax.fori_loop(0, columns, gather, 0)
    pltpu.make_async_copy(back_send.at[me], back_recv.at[me], back_recv_sem).start()

    for m in range(MICRO):
        pipe_copy(m).wait_send()

        def left(turn, carry):
            far = (column + turn) % columns
            pltpu.make_async_copy(send.at[m, far], recv.at[m, far], send_sem.at[m, far]).wait()
            return carry

        lax.fori_loop(1, columns, left, 0)
        pltpu.make_async_copy(
            send.at[m, column, pl.ds(0, depth - 1)],
            recv.at[m, column, pl.ds(0, depth - 1)],
            send_sem.at[m, column],
        ).wait()
    others = pl.ds(0, experts - 1)
    pltpu.make_async_copy(scale_send.at[others], scale_recv.at[others], scale_send_sem).wait()

    pltpu.make_async_copy(back_send, back_recv, back_recv_sem).wait()
    returned = back_recv[...].reshape(experts, LANES)
    slot_grad = [
        jnp.sum(
            slot[k] * dot(returned, named[k], ((0,), (0,)), lax.Precision.HIGHEST),
            axis=0,
            keepdims=True,
        )
        for k in range(TOP)
    ]
    mean = weights[0] * slot_grad[0] + weights[1] * slot_grad[1]
    logit = sum(named[k] * (weights[k] * (slot_grad[k] - mean)) for k in range(TOP))
    logit_ref[...] = logit
    pltpu.make_async_copy(back_send.at[others], back_recv.at[others], back_send_sem).wait()
    pltpu.make_async_copy(hidden, hidden_hbm, store_sem).wait()


def finish(hidden_hbm, logit_hbm, router_hbm, out_hbm, grad_in_hbm, hidden, logit, router, grad_in, sem):
    loads = [
        pltpu.make_async_copy(source, target, sem.at[at])
        for at, (source, target) in enumerate(
            ((hidden_hbm, hidden), (logit_hbm, logit), (router_hbm, router))
        )
    ]
    for load in loads:
        load.start()
    loads[0].wait()
    stores = [
        pltpu.make_async_copy(hidden, out_hbm.at[0], sem.at[3]),
        pltpu.make_async_copy(grad_in, grad_in_hbm.at[0], sem.at[4]),
    ]
    stores[0].start()
    loads[1].wait()
    by_token = logit[...].T
    high = by_token.astype(BF16)
    low = (by_token - high.astype(F32)).astype(BF16)
    loads[2].wait()
    grad_in[...] = (dot(high, router[...]) + dot(low, router[...])).astype(BF16)
    stores[1].start()
    for store in stores:
        store.wait()


def solution(mesh):
    experts = mesh.shape["expert"]

    def on_device(grad_sent, routes, router_probs, saved_hidden, w_down, w_router):
        model_width = grad_sent.shape[2]
        slots, width = saved_hidden.shape[1:]
        tokens = routes.shape[1] // MICRO
        depth = model_width // LANES
        columns = experts // depth
        slab = depth * CAP
        unit = depth * CAP
        in_vmem = pl.BlockSpec(memory_space=pltpu.VMEM)
        in_place = pl.BlockSpec(memory_space=pl.ANY)
        hidden, logit = pl.pallas_call(
            functools.partial(kernel, columns, depth),
            out_shape=(
                jax.ShapeDtypeStruct((slots, width), BF16),
                jax.ShapeDtypeStruct((experts, MICRO * tokens), F32),
            ),
            in_specs=[in_place] * 5,
            out_specs=(in_place, in_vmem),
            scratch_shapes=[
                pltpu.VMEM((TOP, MICRO * tokens), jnp.int32),
                pltpu.VMEM((experts, MICRO * tokens), F32),
                pltpu.VMEM((MICRO, tokens, model_width), BF16),
                pltpu.VMEM((MICRO, experts * CAP, tokens), BF16),
                pltpu.VMEM((slab * depth, slab * depth), BF16),
                pltpu.VMEM((MICRO, columns, depth, unit, LANES), BF16),
                pltpu.VMEM((MICRO, columns, depth, unit, LANES), BF16),
                pltpu.VMEM((slots, width), BF16),
                pltpu.VMEM((width, model_width), BF16),
                pltpu.VMEM((experts, 1, LANES), F32),
                pltpu.VMEM((experts, 1, LANES), F32),
                pltpu.VMEM((experts, LANES), F32),
                pltpu.VMEM((slots, width), BF16),
                pltpu.VMEM((experts, 1, LANES), F32),
                pltpu.VMEM((experts, 1, LANES), F32),
                pltpu.SemaphoreType.DMA((4,)),
                pltpu.SemaphoreType.DMA,
                pltpu.SemaphoreType.DMA((MICRO,)),
                pltpu.SemaphoreType.DMA((MICRO,)),
                pltpu.SemaphoreType.DMA((MICRO, columns)),
                pltpu.SemaphoreType.DMA((MICRO, columns)),
                pltpu.SemaphoreType.DMA,
                pltpu.SemaphoreType.DMA,
                pltpu.SemaphoreType.DMA,
                pltpu.SemaphoreType.DMA,
                pltpu.SemaphoreType.REGULAR,
                pltpu.SemaphoreType.REGULAR((depth.bit_length() - 1,)),
            ],
            compiler_params=pltpu.CompilerParams(
                collective_id=0, has_side_effects=True, vmem_limit_bytes=67043328
            ),
            name="routed_backward",
        )(routes[0].T, router_probs[0].T, grad_sent, saved_hidden, w_down)
        return pl.pallas_call(
            finish,
            out_shape=(
                jax.ShapeDtypeStruct((1, slots, width), BF16),
                jax.ShapeDtypeStruct((1, MICRO * tokens, model_width), BF16),
            ),
            in_specs=[in_place] * 3,
            out_specs=(in_place, in_place),
            scratch_shapes=[
                pltpu.VMEM((slots, width), BF16),
                pltpu.VMEM((experts, MICRO * tokens), F32),
                pltpu.VMEM((experts, model_width), BF16),
                pltpu.VMEM((MICRO * tokens, model_width), BF16),
                pltpu.SemaphoreType.DMA((5,)),
            ],
            compiler_params=pltpu.CompilerParams(vmem_limit_bytes=67043328),
            name="finish",
        )(hidden, logit, w_router.T)

    placed = (
        P("pipe", "expert", None),
        P("pipe", "expert", None),
        P("pipe", "expert", None),
        P("pipe", "expert", None),
        P("expert", None, None),
        P(),
    )
    return jax.shard_map(
        on_device,
        mesh=mesh,
        in_specs=placed,
        out_specs=(P("pipe", "expert", None), P("pipe", "expert", None)),
        check_vma=False,
    )
```

```python
import functools

import jax
import jax.numpy as jnp
from jax import lax
from jax.experimental import pallas as pl
from jax.experimental.pallas import tpu as pltpu
from jax.sharding import PartitionSpec as P

TOP = 2
MICRO = 2
CAP = 3
LANES = 128
F32 = jnp.float32
BF16 = jnp.bfloat16


def iota(shape, axis):
    return lax.broadcasted_iota(jnp.int32, shape, axis)


def split(index, size):
    outer = lax.shift_right_logical(index * ((1 << 16) // size + 1), 16)
    return outer, index - outer * size


def onehot(condition):
    return condition.astype(F32).astype(BF16)


def dot(a, b, dims=((1,), (0,)), precision=None):
    return lax.dot_general(
        a, b, (dims, ((), ())), precision=precision, preferred_element_type=F32
    )


def kernel(
    columns,
    depth,
    routes_hbm,
    probs_hbm,
    grad_hbm,
    saved_hbm,
    weight_hbm,
    hidden_hbm,
    logit_ref,
    routes_ref,
    probs_ref,
    incoming,
    pick,
    order,
    place,
    apart,
    together,
    send,
    recv,
    saved,
    aligned,
    weight,
    scale_send,
    scale_recv,
    hidden,
    placed,
    back_send,
    back_recv,
    load_sem,
    store_sem,
    pipe_send,
    pipe_recv,
    send_sem,
    recv_sem,
    scale_send_sem,
    scale_recv_sem,
    back_send_sem,
    back_recv_sem,
    column_ready,
    level_ready,
):
    experts = columns * depth
    half = depth // 2
    peers = 2 * columns
    rows = MICRO * peers * CAP
    slots = half * rows
    tokens = incoming.shape[1]
    groups = incoming.shape[2] // LANES
    unit = groups * CAP
    size = peers * unit
    first = [2, 3] if half > 3 else [1]
    last = [0] + [w for w in range(half - 1, 0, -1) if w not in first + [1]]
    last += [1] if 1 not in first else []
    waves = first + last
    pipes = lax.axis_size("pipe")
    stage = lax.axis_index("pipe")
    me = lax.axis_index("expert")
    column, level = me // depth, me % depth

    def expert_at(x, z):
        return {"expert": (x % columns) * depth + z % depth}

    def along(distance):
        return [expert_at(column, level + step) for step in (distance, depth - distance)]

    beside = [expert_at(column + step, level) for step in (1, columns - 1)]
    behind = {"pipe": (stage + pipes - 1) % pipes}
    ahead = {"pipe": (stage + 1) % pipes}

    barrier = pltpu.get_barrier_semaphore()
    for device in along(1) + beside + [behind, ahead]:
        pl.semaphore_signal(barrier, inc=1, device_id=device)
    loads = [
        pltpu.make_async_copy(source, target, load_sem.at[at])
        for at, (source, target) in enumerate(
            (
                (routes_hbm, routes_ref),
                (probs_hbm, probs_ref),
                (saved_hbm.at[0], saved),
                (weight_hbm.at[0], weight),
            )
        )
    ]
    for load in loads:
        load.start()
    pl.semaphore_wait(barrier, 6)

    def pipe_copy(m):
        return pltpu.make_async_remote_copy(
            src_ref=grad_hbm.at[0, pl.ds(m * tokens, tokens)],
            dst_ref=incoming.at[m],
            send_sem=pipe_send.at[m],
            recv_sem=pipe_recv.at[m],
            device_id=behind,
        )

    for m in range(MICRO):
        pipe_copy(m).start()
    for device in beside:
        pl.semaphore_signal(column_ready, inc=1, device_id=device)

    loads[0].wait()
    loads[1].wait()
    all_tokens = MICRO * tokens
    expert_row = iota((experts, all_tokens), 0)
    named = [(expert_row == routes_ref[k : k + 1, :]).astype(F32) for k in range(TOP)]
    probs = probs_ref[...]
    chosen = [jnp.sum(named[k] * probs, axis=0, keepdims=True) for k in range(TOP)]
    total = chosen[0] + chosen[1]
    weights = [chosen[k] / total for k in range(TOP)]
    before, after = iota((all_tokens, all_tokens), 0), iota((all_tokens, all_tokens), 1)
    earlier = (before < after) & ((before >= tokens) == (after >= tokens))
    seen = dot((named[0] + named[1]).astype(BF16), onehot(earlier))
    rank = [jnp.sum(named[k] * seen, axis=0, keepdims=True) for k in range(TOP)]
    row = [routes_ref[k : k + 1, :].astype(F32) * CAP + rank[k] for k in range(TOP)]

    rounds = [1] + [1 << at for at in range(depth.bit_length() - 2)]

    def tell(at):
        for device in along(rounds[at]):
            pl.semaphore_signal(level_ready.at[at], inc=1, device_id=device)

    def hear(at):
        pl.semaphore_wait(level_ready.at[at], 2)

    pl.semaphore_wait(column_ready, 2)
    tell(0)

    def levels(wave, sign):
        other = jnp.where(wave == 0, half, wave)
        return level + depth + sign * wave, level + depth - sign * other

    def peer_of(wave, peer, sign):
        direct, opposite = levels(wave, sign)
        other = (peer >= columns).astype(jnp.int32)
        z = jnp.where(other == 1, opposite, direct)
        z = z - jnp.where(z >= 2 * depth, 2 * depth, jnp.where(z >= depth, depth, 0))
        return (peer - other * columns) * depth + z

    wave, rest = split(iota((slots // MICRO, 1), 0), peers * CAP)
    peer, own = split(rest, CAP)
    wanted = (peer_of(wave, peer, 1) * CAP + own).astype(F32)
    for m in range(MICRO):
        part = [row[k][:, m * tokens : (m + 1) * tokens] for k in range(TOP)]
        pick[m] = onehot((wanted == part[0]) | (wanted == part[1])).reshape(half, peers * CAP, tokens)
    hear(0)
    tell(1)
    micro = (iota((1, all_tokens), 1) >= tokens).astype(F32)
    lane_row = iota((LANES, all_tokens), 0).astype(F32)
    slot = [(lane_row == micro * CAP + rank[k]).astype(F32) for k in range(TOP)]
    p, inner = split(iota((size, 1), 0), unit)
    j, own = split(inner, CAP)
    apart[...] = onehot(iota((size, size), 1) == j * (peers * CAP) + p * CAP + own)
    for at in range(1, len(rounds) - 1):
        hear(at)
        tell(at + 1)
    scales = sum(
        dot(
            named[k].astype(BF16),
            (slot[k] * weights[k].astype(BF16).astype(F32)).astype(BF16),
            ((1,), (1,)),
        )
        for k in range(TOP)
    )
    wave, peer = split(iota((half * peers, 1), 0), peers)
    turned = onehot(iota((half * peers, experts), 1) == peer_of(wave, peer, 1))
    scale_send[...] = dot(turned, scales.astype(BF16)).reshape(half, peers, 1, LANES)

    def wave_at(turn):
        wave = waves[0]
        for at in range(1, half):
            wave = jnp.where(turn == at, waves[at], wave)
        return wave

    def visit(wave, sign, step):
        direct, opposite = levels(wave, sign)
        other = step % 2
        x = (column + step // 2) % columns
        z = jnp.where(other == 1, opposite, direct)
        return other * columns + x, other * columns + column, expert_at(x, z)

    def row_copy(wave, m, step):
        there, here, device = visit(wave, 1, step)
        return pltpu.make_async_remote_copy(
            src_ref=send.at[wave, m, there],
            dst_ref=recv.at[wave, m, here],
            send_sem=send_sem.at[wave],
            recv_sem=recv_sem.at[wave],
            device_id=device,
        )

    def scale_copy(wave, step):
        there, here, device = visit(wave, 1, step)
        return pltpu.make_async_remote_copy(
            src_ref=scale_send.at[wave, there],
            dst_ref=scale_recv.at[wave, here],
            send_sem=scale_send_sem.at[wave],
            recv_sem=scale_recv_sem.at[wave],
            device_id=device,
        )

    def back_copy(wave, step):
        there, _, device = visit(wave, -1, step)
        return pltpu.make_async_remote_copy(
            src_ref=back_send.at[wave, there],
            dst_ref=back_recv.at[me],
            send_sem=back_send_sem,
            recv_sem=back_recv_sem,
            device_id=device,
        )

    def others(wave):
        return jnp.where(wave == 0, 1, 0)

    def spread(m, turn):
        wave = wave_at(turn)
        picked = dot(pick[m, wave], incoming[m])
        stacked = jnp.concatenate(
            [picked[:, j * LANES : (j + 1) * LANES] for j in range(groups)], axis=0
        ).astype(BF16)
        send[wave, m] = dot(apart[...], stacked).astype(BF16).reshape(peers, unit, LANES)

        def out(step, carry):
            row_copy(wave, m, step).start()
            return carry

        lax.fori_loop(others(wave), peers, out, 0)

    def spread_first(m):
        def body(turn, carry):
            spread(m, turn)
            return carry

        lax.fori_loop(0, len(first), body, 0)

    def spread_last(index, carry):
        turn, m = index // MICRO, index % MICRO
        spread(m, turn)
        return carry

    def spread_scales(index, carry):
        wave, step = index // peers, index % peers
        scale_copy(wave, step).start()
        return carry

    for m in range(MICRO):
        pipe_copy(m).wait_recv()
        spread_first(m)
    hear(len(rounds) - 1)
    lax.fori_loop(1, half * peers, spread_scales, 0)
    lax.fori_loop(len(first) * MICRO, half * MICRO, spread_last, 0)
    pltpu.make_async_copy(scale_send.at[0, column], scale_recv.at[0, column], scale_recv_sem.at[0]).start()
    for m in range(MICRO):
        pltpu.make_async_copy(
            send.at[0, m, column], recv.at[0, m, column], recv_sem.at[0]
        ).start()

    def natural(index):
        wave, rest = split(index, rows)
        m, rest = split(rest, peers * CAP)
        peer, own = split(rest, CAP)
        return (m * experts + peer_of(wave, peer, -1)) * CAP + own

    order[...] = onehot(iota((slots, slots), 1) == natural(iota((slots, 1), 0)))
    place[...] = onehot(iota((slots, slots), 0) == natural(iota((1, slots), 1)))
    j, inner = split(iota((MICRO * size, 1), 0), rows)
    m, inner = split(inner, peers * CAP)
    p, own = split(inner, CAP)
    together[...] = onehot(
        iota((MICRO * size, MICRO * size), 1) == m * size + p * unit + j * CAP + own
    )

    def peer_and_slot(line):
        m, inner = split(line, peers * CAP)
        p, own = split(inner, CAP)
        return p, m * CAP + own

    ours = iota((rows, LANES), 1) == peer_and_slot(iota((rows, LANES), 0))[1]
    holder = onehot(peer_and_slot(iota((rows, peers), 0))[0] == iota((rows, peers), 1))
    holder_t = (peer_and_slot(iota((peers, rows), 1))[0] == iota((peers, rows), 0)).astype(F32)
    loads[2].wait()
    aligned[...] = dot(order[...], saved[...]).astype(BF16)
    loads[3].wait()

    def gather(turn, carry):
        wave = wave_at(turn)
        start = pl.multiple_of(wave * rows, 16)
        held = aligned[pl.ds(start, rows), :].astype(F32)
        pltpu.make_async_copy(
            scale_send.at[wave], scale_recv.at[wave], scale_recv_sem.at[wave]
        ).wait()
        all_scales = scale_recv[wave].reshape(peers, LANES).astype(BF16)
        scale = jnp.sum(jnp.where(ours, dot(holder, all_scales), 0.0), axis=1, keepdims=True)
        pltpu.make_async_copy(send.at[wave], recv.at[wave], recv_sem.at[wave]).wait()
        mixed = dot(together[...], recv[wave].reshape(MICRO * size, LANES)).astype(BF16)
        flat = jnp.concatenate(
            [mixed[j * rows : (j + 1) * rows] for j in range(groups)], axis=1
        )
        grad = dot(flat, weight[...], ((1,), (1,)))
        route_grad = jnp.sum(grad * held, axis=1, keepdims=True)
        sums = dot(holder_t, jnp.where(ours, route_grad, 0.0), precision=lax.Precision.HIGHEST)
        back_send[wave] = sums.reshape(peers, 1, LANES)

        def back(step, inner_carry):
            back_copy(wave, step).start()
            return inner_carry

        lax.fori_loop(others(wave), peers, back, 0)
        hidden[pl.ds(start, rows), :] = (scale * grad).astype(BF16)
        return carry

    lax.fori_loop(0, half, gather, 0)
    pltpu.make_async_copy(back_send.at[0, column], back_recv.at[me], back_recv_sem).start()
    placed[...] = dot(place[...], hidden[...]).astype(BF16)
    pltpu.make_async_copy(placed, hidden_hbm, store_sem).start()

    for m in range(MICRO):
        pipe_copy(m).wait_send()

    def left(wave, carry):
        pltpu.make_async_copy(send.at[wave], recv.at[wave], send_sem.at[wave]).wait()
        pltpu.make_async_copy(
            scale_send.at[wave], scale_recv.at[wave], scale_send_sem.at[wave]
        ).wait()
        return carry

    lax.fori_loop(1, half, left, 0)
    remote = pl.ds(0, peers - 1)
    both = pl.ds(0, MICRO)
    pltpu.make_async_copy(
        send.at[0, both, remote], recv.at[0, both, remote], send_sem.at[0]
    ).wait()
    pltpu.make_async_copy(
        scale_send.at[0, remote], scale_recv.at[0, remote], scale_send_sem.at[0]
    ).wait()
    pltpu.make_async_copy(back_recv, back_recv, back_recv_sem).wait()
    returned = back_recv[...].reshape(experts, LANES)
    slot_grad = [
        jnp.sum(
            slot[k] * dot(returned, named[k], ((0,), (0,)), lax.Precision.HIGHEST),
            axis=0,
            keepdims=True,
        )
        for k in range(TOP)
    ]
    mean = weights[0] * slot_grad[0] + weights[1] * slot_grad[1]
    logit = sum(named[k] * (weights[k] * (slot_grad[k] - mean)) for k in range(TOP))
    logit_ref[...] = logit
    away = pl.ds(0, experts - 1)
    pltpu.make_async_copy(back_recv.at[away], back_recv.at[away], back_send_sem).wait()
    pltpu.make_async_copy(placed, hidden_hbm, store_sem).wait()


def finish(hidden_hbm, logit_hbm, router_hbm, out_hbm, grad_in_hbm, hidden, logit, router, grad_in, sem):
    loads = [
        pltpu.make_async_copy(source, target, sem.at[at])
        for at, (source, target) in enumerate(
            ((hidden_hbm, hidden), (logit_hbm, logit), (router_hbm, router))
        )
    ]
    for load in loads:
        load.start()
    loads[0].wait()
    stores = [
        pltpu.make_async_copy(hidden, out_hbm.at[0], sem.at[3]),
        pltpu.make_async_copy(grad_in, grad_in_hbm.at[0], sem.at[4]),
    ]
    stores[0].start()
    loads[1].wait()
    by_token = logit[...].T
    high = by_token.astype(BF16)
    low = (by_token - high.astype(F32)).astype(BF16)
    loads[2].wait()
    grad_in[...] = (dot(high, router[...]) + dot(low, router[...])).astype(BF16)
    stores[1].start()
    for store in stores:
        store.wait()


def solution(mesh):
    experts = mesh.shape["expert"]

    def on_device(grad_sent, routes, router_probs, saved_hidden, w_down, w_router):
        model_width = grad_sent.shape[2]
        slots, width = saved_hidden.shape[1:]
        tokens = routes.shape[1] // MICRO
        depth = model_width // LANES
        columns = experts // depth
        half = depth // 2
        peers = 2 * columns
        unit = model_width // LANES * CAP
        in_vmem = pl.BlockSpec(memory_space=pltpu.VMEM)
        in_place = pl.BlockSpec(memory_space=pl.ANY)
        hidden, logit = pl.pallas_call(
            functools.partial(kernel, columns, depth),
            out_shape=(
                jax.ShapeDtypeStruct((slots, width), BF16),
                jax.ShapeDtypeStruct((experts, MICRO * tokens), F32),
            ),
            in_specs=[in_place] * 5,
            out_specs=(in_place, in_vmem),
            scratch_shapes=[
                pltpu.VMEM((TOP, MICRO * tokens), jnp.int32),
                pltpu.VMEM((experts, MICRO * tokens), F32),
                pltpu.VMEM((MICRO, tokens, model_width), BF16),
                pltpu.VMEM((MICRO, half, peers * CAP, tokens), BF16),
                pltpu.VMEM((slots, slots), BF16),
                pltpu.VMEM((slots, slots), BF16),
                pltpu.VMEM((peers * unit, peers * unit), BF16),
                pltpu.VMEM((MICRO * peers * unit, MICRO * peers * unit), BF16),
                pltpu.VMEM((half, MICRO, peers, unit, LANES), BF16),
                pltpu.VMEM((half, MICRO, peers, unit, LANES), BF16),
                pltpu.VMEM((slots, width), BF16),
                pltpu.VMEM((slots, width), BF16),
                pltpu.VMEM((width, model_width), BF16),
                pltpu.VMEM((half, peers, 1, LANES), F32),
                pltpu.VMEM((half, peers, 1, LANES), F32),
                pltpu.VMEM((slots, width), BF16),
                pltpu.VMEM((slots, width), BF16),
                pltpu.VMEM((half, peers, 1, LANES), F32),
                pltpu.VMEM((experts, 1, LANES), F32),
                pltpu.SemaphoreType.DMA((4,)),
                pltpu.SemaphoreType.DMA,
                pltpu.SemaphoreType.DMA((MICRO,)),
                pltpu.SemaphoreType.DMA((MICRO,)),
                pltpu.SemaphoreType.DMA((half,)),
                pltpu.SemaphoreType.DMA((half,)),
                pltpu.SemaphoreType.DMA((half,)),
                pltpu.SemaphoreType.DMA((half,)),
                pltpu.SemaphoreType.DMA,
                pltpu.SemaphoreType.DMA,
                pltpu.SemaphoreType.REGULAR,
                pltpu.SemaphoreType.REGULAR((depth.bit_length() - 1,)),
            ],
            compiler_params=pltpu.CompilerParams(
                collective_id=0, has_side_effects=True, vmem_limit_bytes=67043328
            ),
            name="routed_backward",
        )(routes[0].T, router_probs[0].T, grad_sent, saved_hidden, w_down)
        return pl.pallas_call(
            finish,
            out_shape=(
                jax.ShapeDtypeStruct((1, slots, width), BF16),
                jax.ShapeDtypeStruct((1, MICRO * tokens, model_width), BF16),
            ),
            in_specs=[in_place] * 3,
            out_specs=(in_place, in_place),
            scratch_shapes=[
                pltpu.VMEM((slots, width), BF16),
                pltpu.VMEM((experts, MICRO * tokens), F32),
                pltpu.VMEM((experts, model_width), BF16),
                pltpu.VMEM((MICRO * tokens, model_width), BF16),
                pltpu.SemaphoreType.DMA((5,)),
            ],
            compiler_params=pltpu.CompilerParams(vmem_limit_bytes=67043328),
            name="finish",
        )(hidden, logit, w_router.T)

    placed = (
        P("pipe", "expert", None),
        P("pipe", "expert", None),
        P("pipe", "expert", None),
        P("pipe", "expert", None),
        P("expert", None, None),
        P(),
    )
    return jax.shard_map(
        on_device,
        mesh=mesh,
        in_specs=placed,
        out_specs=(P("pipe", "expert", None), P("pipe", "expert", None)),
        check_vma=False,
    )
```

```python
import functools

import jax
import jax.numpy as jnp
from jax import lax
from jax.experimental import pallas as pl
from jax.experimental.pallas import tpu as pltpu
from jax.sharding import PartitionSpec as P

TOP = 2
MICRO = 2
CAP = 3
LANES = 128
F32 = jnp.float32
BF16 = jnp.bfloat16


def iota(shape, axis):
    return lax.broadcasted_iota(jnp.int32, shape, axis)


def split(index, size):
    outer = lax.shift_right_logical(index * ((1 << 16) // size + 1), 16)
    return outer, index - outer * size


def onehot(condition):
    return condition.astype(F32).astype(BF16)


def dot(a, b, dims=((1,), (0,)), precision=None):
    return lax.dot_general(
        a, b, (dims, ((), ())), precision=precision, preferred_element_type=F32
    )


def kernel(
    columns,
    depth,
    routes_hbm,
    probs_hbm,
    grad_hbm,
    saved_hbm,
    weight_hbm,
    hidden_hbm,
    logit_ref,
    routes_ref,
    probs_ref,
    incoming,
    pick,
    order,
    place,
    apart,
    together,
    send,
    recv,
    saved,
    aligned,
    weight,
    scale_send,
    scale_recv,
    hidden,
    placed,
    back_send,
    back_recv,
    load_sem,
    store_sem,
    pipe_send,
    pipe_recv,
    send_sem,
    recv_sem,
    scale_send_sem,
    scale_recv_sem,
    back_send_sem,
    back_recv_sem,
    column_ready,
    level_ready,
):
    experts = columns * depth
    half = depth // 2
    peers = 2 * columns
    rows = MICRO * peers * CAP
    slots = half * rows
    tokens = incoming.shape[1]
    groups = incoming.shape[2] // LANES
    unit = groups * CAP
    size = peers * unit
    first = [2, 3] if half > 3 else [1]
    last = [0] + [w for w in range(half - 1, 0, -1) if w not in first + [1]]
    last += [1] if 1 not in first else []
    waves = first + last
    pipes = lax.axis_size("pipe")
    stage = lax.axis_index("pipe")
    me = lax.axis_index("expert")
    column, level = me // depth, me % depth

    def expert_at(x, z):
        return {"expert": (x % columns) * depth + z % depth}

    def along(distance):
        return [expert_at(column, level + step) for step in (distance, depth - distance)]

    beside = [expert_at(column + step, level) for step in (1, columns - 1)]
    behind = {"pipe": (stage + pipes - 1) % pipes}
    ahead = {"pipe": (stage + 1) % pipes}

    barrier = pltpu.get_barrier_semaphore()
    for device in along(1) + beside + [behind, ahead]:
        pl.semaphore_signal(barrier, inc=1, device_id=device)
    loads = [
        pltpu.make_async_copy(source, target, load_sem.at[at])
        for at, (source, target) in enumerate(
            (
                (routes_hbm, routes_ref),
                (probs_hbm, probs_ref),
                (saved_hbm.at[0], saved),
                (weight_hbm.at[0], weight),
            )
        )
    ]
    for load in loads:
        load.start()
    pl.semaphore_wait(barrier, 6)

    def pipe_copy(m):
        return pltpu.make_async_remote_copy(
            src_ref=grad_hbm.at[0, pl.ds(m * tokens, tokens)],
            dst_ref=incoming.at[m],
            send_sem=pipe_send.at[m],
            recv_sem=pipe_recv.at[m],
            device_id=behind,
        )

    for m in range(MICRO):
        pipe_copy(m).start()
    for device in beside:
        pl.semaphore_signal(column_ready, inc=1, device_id=device)

    loads[0].wait()
    loads[1].wait()
    all_tokens = MICRO * tokens
    expert_row = iota((experts, all_tokens), 0)
    named = [(expert_row == routes_ref[k : k + 1, :]).astype(F32) for k in range(TOP)]
    probs = probs_ref[...]
    chosen = [jnp.sum(named[k] * probs, axis=0, keepdims=True) for k in range(TOP)]
    total = chosen[0] + chosen[1]
    weights = [chosen[k] / total for k in range(TOP)]
    before, after = iota((all_tokens, all_tokens), 0), iota((all_tokens, all_tokens), 1)
    earlier = (before < after) & ((before >= tokens) == (after >= tokens))
    seen = dot((named[0] + named[1]).astype(BF16), onehot(earlier))
    rank = [jnp.sum(named[k] * seen, axis=0, keepdims=True) for k in range(TOP)]
    row = [routes_ref[k : k + 1, :].astype(F32) * CAP + rank[k] for k in range(TOP)]

    rounds = [1] + [1 << at for at in range(depth.bit_length() - 2)]

    def tell(at):
        for device in along(rounds[at]):
            pl.semaphore_signal(level_ready.at[at], inc=1, device_id=device)

    def hear(at):
        pl.semaphore_wait(level_ready.at[at], 2)

    pl.semaphore_wait(column_ready, 2)
    tell(0)

    def levels(wave, sign):
        other = jnp.where(wave == 0, half, wave)
        return level + depth + sign * wave, level + depth - sign * other

    def peer_of(wave, peer, sign):
        direct, opposite = levels(wave, sign)
        other = (peer >= columns).astype(jnp.int32)
        z = jnp.where(other == 1, opposite, direct)
        z = z - jnp.where(z >= 2 * depth, 2 * depth, jnp.where(z >= depth, depth, 0))
        return (peer - other * columns) * depth + z

    wave, rest = split(iota((slots // MICRO, 1), 0), peers * CAP)
    peer, own = split(rest, CAP)
    wanted = (peer_of(wave, peer, 1) * CAP + own).astype(F32)
    for m in range(MICRO):
        part = [row[k][:, m * tokens : (m + 1) * tokens] for k in range(TOP)]
        pick[m] = onehot((wanted == part[0]) | (wanted == part[1])).reshape(half, peers * CAP, tokens)
    hear(0)
    tell(1)
    micro = (iota((1, all_tokens), 1) >= tokens).astype(F32)
    lane_row = iota((LANES, all_tokens), 0).astype(F32)
    slot = [(lane_row == micro * CAP + rank[k]).astype(F32) for k in range(TOP)]
    p, inner = split(iota((size, 1), 0), unit)
    j, own = split(inner, CAP)
    apart[...] = onehot(iota((size, size), 1) == j * (peers * CAP) + p * CAP + own)
    for at in range(1, len(rounds) - 1):
        hear(at)
        tell(at + 1)
    scales = sum(
        dot(
            named[k].astype(BF16),
            (slot[k] * weights[k].astype(BF16).astype(F32)).astype(BF16),
            ((1,), (1,)),
        )
        for k in range(TOP)
    )
    wave, peer = split(iota((half * peers, 1), 0), peers)
    turned = onehot(iota((half * peers, experts), 1) == peer_of(wave, peer, 1))
    scale_send[...] = dot(turned, scales.astype(BF16)).reshape(half, peers, 1, LANES)

    def wave_at(turn):
        wave = waves[0]
        for at in range(1, half):
            wave = jnp.where(turn == at, waves[at], wave)
        return wave

    def visit(wave, sign, step):
        direct, opposite = levels(wave, sign)
        other = step % 2
        x = (column + step // 2) % columns
        z = jnp.where(other == 1, opposite, direct)
        return other * columns + x, other * columns + column, expert_at(x, z)

    def row_copy(wave, m, step):
        there, here, device = visit(wave, 1, step)
        return pltpu.make_async_remote_copy(
            src_ref=send.at[wave, m, there],
            dst_ref=recv.at[wave, m, here],
            send_sem=send_sem.at[wave],
            recv_sem=recv_sem.at[wave],
            device_id=device,
        )

    def scale_copy(wave, step):
        there, here, device = visit(wave, 1, step)
        return pltpu.make_async_remote_copy(
            src_ref=scale_send.at[wave, there],
            dst_ref=scale_recv.at[wave, here],
            send_sem=scale_send_sem.at[wave],
            recv_sem=scale_recv_sem.at[wave],
            device_id=device,
        )

    def back_copy(wave, step):
        there, _, device = visit(wave, -1, step)
        return pltpu.make_async_remote_copy(
            src_ref=back_send.at[wave, there],
            dst_ref=back_recv.at[me],
            send_sem=back_send_sem,
            recv_sem=back_recv_sem,
            device_id=device,
        )

    def others(wave):
        return jnp.where(wave == 0, 1, 0)

    def spread(m, turn):
        wave = wave_at(turn)
        picked = dot(pick[m, wave], incoming[m])
        stacked = jnp.concatenate(
            [picked[:, j * LANES : (j + 1) * LANES] for j in range(groups)], axis=0
        ).astype(BF16)
        send[wave, m] = dot(apart[...], stacked).astype(BF16).reshape(peers, unit, LANES)

        def out(step, carry):
            row_copy(wave, m, step).start()
            return carry

        lax.fori_loop(others(wave), peers, out, 0)

    def spread_first(m):
        def body(turn, carry):
            spread(m, turn)
            return carry

        lax.fori_loop(0, len(first), body, 0)

    def spread_last(index, carry):
        turn, m = index // MICRO, index % MICRO
        spread(m, turn)
        return carry

    def spread_scales(index, carry):
        wave, step = index // peers, index % peers
        scale_copy(wave, step).start()
        return carry

    for m in range(MICRO):
        pipe_copy(m).wait_recv()
        spread_first(m)
    hear(len(rounds) - 1)
    lax.fori_loop(1, half * peers, spread_scales, 0)
    lax.fori_loop(len(first) * MICRO, half * MICRO, spread_last, 0)
    pltpu.make_async_copy(scale_send.at[0, column], scale_recv.at[0, column], scale_recv_sem.at[0]).start()
    for m in range(MICRO):
        pltpu.make_async_copy(
            send.at[0, m, column], recv.at[0, m, column], recv_sem.at[0]
        ).start()

    def natural(index):
        wave, rest = split(index, rows)
        m, rest = split(rest, peers * CAP)
        peer, own = split(rest, CAP)
        return (m * experts + peer_of(wave, peer, -1)) * CAP + own

    order[...] = onehot(iota((slots, slots), 1) == natural(iota((slots, 1), 0)))
    place[...] = onehot(iota((slots, slots), 0) == natural(iota((1, slots), 1)))
    j, inner = split(iota((size, 1), 0), peers * CAP)
    p, own = split(inner, CAP)
    together[...] = onehot(iota((size, size), 1) == p * unit + j * CAP + own)

    def peer_and_slot(line):
        m, inner = split(line, peers * CAP)
        p, own = split(inner, CAP)
        return p, m * CAP + own

    ours = iota((rows, LANES), 1) == peer_and_slot(iota((rows, LANES), 0))[1]
    holder = onehot(peer_and_slot(iota((rows, peers), 0))[0] == iota((rows, peers), 1))
    holder_t = (peer_and_slot(iota((peers, rows), 1))[0] == iota((peers, rows), 0)).astype(F32)
    loads[2].wait()
    aligned[...] = dot(order[...], saved[...]).astype(BF16)
    loads[3].wait()

    def gather(turn, carry):
        wave = wave_at(turn)
        start = pl.multiple_of(wave * rows, 16)
        held = aligned[pl.ds(start, rows), :].astype(F32)
        pltpu.make_async_copy(
            scale_send.at[wave], scale_recv.at[wave], scale_recv_sem.at[wave]
        ).wait()
        all_scales = scale_recv[wave].reshape(peers, LANES).astype(BF16)
        scale = jnp.sum(jnp.where(ours, dot(holder, all_scales), 0.0), axis=1, keepdims=True)
        pltpu.make_async_copy(send.at[wave], recv.at[wave], recv_sem.at[wave]).wait()
        parts = []
        for m in range(MICRO):
            mixed = dot(together[...], recv[wave, m].reshape(size, LANES))
            pieces = [mixed[j * peers * CAP : (j + 1) * peers * CAP] for j in range(groups)]
            parts.append(jnp.concatenate(pieces, axis=1))
        flat = jnp.concatenate(parts, axis=0).astype(BF16)
        grad = dot(flat, weight[...], ((1,), (1,)))
        route_grad = jnp.sum(grad * held, axis=1, keepdims=True)
        sums = dot(holder_t, jnp.where(ours, route_grad, 0.0), precision=lax.Precision.HIGHEST)
        back_send[wave] = sums.reshape(peers, 1, LANES)

        def back(step, inner_carry):
            back_copy(wave, step).start()
            return inner_carry

        lax.fori_loop(others(wave), peers, back, 0)
        hidden[pl.ds(start, rows), :] = (scale * grad).astype(BF16)
        return carry

    lax.fori_loop(0, half, gather, 0)
    pltpu.make_async_copy(back_send.at[0, column], back_recv.at[me], back_recv_sem).start()
    placed[...] = dot(place[...], hidden[...]).astype(BF16)
    pltpu.make_async_copy(placed, hidden_hbm, store_sem).start()

    for m in range(MICRO):
        pipe_copy(m).wait_send()

    def left(wave, carry):
        pltpu.make_async_copy(send.at[wave], recv.at[wave], send_sem.at[wave]).wait()
        pltpu.make_async_copy(
            scale_send.at[wave], scale_recv.at[wave], scale_send_sem.at[wave]
        ).wait()
        return carry

    lax.fori_loop(1, half, left, 0)
    remote = pl.ds(0, peers - 1)
    both = pl.ds(0, MICRO)
    pltpu.make_async_copy(
        send.at[0, both, remote], recv.at[0, both, remote], send_sem.at[0]
    ).wait()
    pltpu.make_async_copy(
        scale_send.at[0, remote], scale_recv.at[0, remote], scale_send_sem.at[0]
    ).wait()
    pltpu.make_async_copy(back_recv, back_recv, back_recv_sem).wait()
    returned = back_recv[...].reshape(experts, LANES)
    slot_grad = [
        jnp.sum(
            slot[k] * dot(returned, named[k], ((0,), (0,)), lax.Precision.HIGHEST),
            axis=0,
            keepdims=True,
        )
        for k in range(TOP)
    ]
    mean = weights[0] * slot_grad[0] + weights[1] * slot_grad[1]
    logit = sum(named[k] * (weights[k] * (slot_grad[k] - mean)) for k in range(TOP))
    logit_ref[...] = logit
    away = pl.ds(0, experts - 1)
    pltpu.make_async_copy(back_recv.at[away], back_recv.at[away], back_send_sem).wait()
    pltpu.make_async_copy(placed, hidden_hbm, store_sem).wait()


def finish(hidden_hbm, logit_hbm, router_hbm, out_hbm, grad_in_hbm, hidden, logit, router, grad_in, sem):
    loads = [
        pltpu.make_async_copy(source, target, sem.at[at])
        for at, (source, target) in enumerate(
            ((hidden_hbm, hidden), (logit_hbm, logit), (router_hbm, router))
        )
    ]
    for load in loads:
        load.start()
    loads[0].wait()
    stores = [
        pltpu.make_async_copy(hidden, out_hbm.at[0], sem.at[3]),
        pltpu.make_async_copy(grad_in, grad_in_hbm.at[0], sem.at[4]),
    ]
    stores[0].start()
    loads[1].wait()
    by_token = logit[...].T
    high = by_token.astype(BF16)
    low = (by_token - high.astype(F32)).astype(BF16)
    loads[2].wait()
    grad_in[...] = (dot(high, router[...]) + dot(low, router[...])).astype(BF16)
    stores[1].start()
    for store in stores:
        store.wait()


def solution(mesh):
    experts = mesh.shape["expert"]

    def on_device(grad_sent, routes, router_probs, saved_hidden, w_down, w_router):
        model_width = grad_sent.shape[2]
        slots, width = saved_hidden.shape[1:]
        tokens = routes.shape[1] // MICRO
        depth = model_width // LANES
        columns = experts // depth
        half = depth // 2
        peers = 2 * columns
        unit = model_width // LANES * CAP
        in_vmem = pl.BlockSpec(memory_space=pltpu.VMEM)
        in_place = pl.BlockSpec(memory_space=pl.ANY)
        hidden, logit = pl.pallas_call(
            functools.partial(kernel, columns, depth),
            out_shape=(
                jax.ShapeDtypeStruct((slots, width), BF16),
                jax.ShapeDtypeStruct((experts, MICRO * tokens), F32),
            ),
            in_specs=[in_place] * 5,
            out_specs=(in_place, in_vmem),
            scratch_shapes=[
                pltpu.VMEM((TOP, MICRO * tokens), jnp.int32),
                pltpu.VMEM((experts, MICRO * tokens), F32),
                pltpu.VMEM((MICRO, tokens, model_width), BF16),
                pltpu.VMEM((MICRO, half, peers * CAP, tokens), BF16),
                pltpu.VMEM((slots, slots), BF16),
                pltpu.VMEM((slots, slots), BF16),
                pltpu.VMEM((peers * unit, peers * unit), BF16),
                pltpu.VMEM((peers * unit, peers * unit), BF16),
                pltpu.VMEM((half, MICRO, peers, unit, LANES), BF16),
                pltpu.VMEM((half, MICRO, peers, unit, LANES), BF16),
                pltpu.VMEM((slots, width), BF16),
                pltpu.VMEM((slots, width), BF16),
                pltpu.VMEM((width, model_width), BF16),
                pltpu.VMEM((half, peers, 1, LANES), F32),
                pltpu.VMEM((half, peers, 1, LANES), F32),
                pltpu.VMEM((slots, width), BF16),
                pltpu.VMEM((slots, width), BF16),
                pltpu.VMEM((half, peers, 1, LANES), F32),
                pltpu.VMEM((experts, 1, LANES), F32),
                pltpu.SemaphoreType.DMA((4,)),
                pltpu.SemaphoreType.DMA,
                pltpu.SemaphoreType.DMA((MICRO,)),
                pltpu.SemaphoreType.DMA((MICRO,)),
                pltpu.SemaphoreType.DMA((half,)),
                pltpu.SemaphoreType.DMA((half,)),
                pltpu.SemaphoreType.DMA((half,)),
                pltpu.SemaphoreType.DMA((half,)),
                pltpu.SemaphoreType.DMA,
                pltpu.SemaphoreType.DMA,
                pltpu.SemaphoreType.REGULAR,
                pltpu.SemaphoreType.REGULAR((depth.bit_length() - 1,)),
            ],
            compiler_params=pltpu.CompilerParams(
                collective_id=0, has_side_effects=True, vmem_limit_bytes=67043328
            ),
            name="routed_backward",
        )(routes[0].T, router_probs[0].T, grad_sent, saved_hidden, w_down)
        return pl.pallas_call(
            finish,
            out_shape=(
                jax.ShapeDtypeStruct((1, slots, width), BF16),
                jax.ShapeDtypeStruct((1, MICRO * tokens, model_width), BF16),
            ),
            in_specs=[in_place] * 3,
            out_specs=(in_place, in_place),
            scratch_shapes=[
                pltpu.VMEM((slots, width), BF16),
                pltpu.VMEM((experts, MICRO * tokens), F32),
                pltpu.VMEM((experts, model_width), BF16),
                pltpu.VMEM((MICRO * tokens, model_width), BF16),
                pltpu.SemaphoreType.DMA((5,)),
            ],
            compiler_params=pltpu.CompilerParams(vmem_limit_bytes=67043328),
            name="finish",
        )(hidden, logit, w_router.T)

    placed = (
        P("pipe", "expert", None),
        P("pipe", "expert", None),
        P("pipe", "expert", None),
        P("pipe", "expert", None),
        P("expert", None, None),
        P(),
    )
    return jax.shard_map(
        on_device,
        mesh=mesh,
        in_specs=placed,
        out_specs=(P("pipe", "expert", None), P("pipe", "expert", None)),
        check_vma=False,
    )
```
